32 devices in a mesh: grp: 2 (over y), pair: 4 (over z), aux: 2 (over x), rep: 2 (over core).
Axes of the slice: x: 2, y: 2, z: 4, core: 2. Of those that a mesh axis runs over, the one named last changes fastest.
Arguments:
- three_center: bfloat16 [5120, 4, 8000], P(('grp', 'aux', 'rep', 'pair')), parts along dimension 0, may hold values from -0.050591038 to 0.050591038
- eps_occ: float32 [8], P('grp'), parts along dimension 0, may hold values from -1.2 to -0.4
- eps_virt: float32 [16000], P(('grp', 'pair')), parts along dimension 0, may hold values from 0.2 to 3
- freq: float32 [2], P('grp'), parts along dimension 0, may hold values from 0.2 to 2
Outputs:
- polar: float32 [5120, 2560], P(('grp', 'aux', 'rep'), 'pair'), parts along dimension 0
The draws below stay inside these ranges and needn't reach their ends.
There are 2 independent parts, one for each index of `grp`. The reference program is written for one: setup_inputs(seed, part) draws one part's arguments, and reference() takes and returns one part's arrays. A program takes and returns all parts, laid end to end along the dimension named above; each array names one. Nothing has to cross between parts.
All inputs are finite; a program needn't handle non-finite values.
Results may differ from the reference program's by a relative error of at most 0.0003.
Values may be sent and summed in bfloat16 or wider, within the bound.
A program may use at most 192 MiB of HBM per device.

```python
import math
import jax
import jax.numpy as jnp
from jax import lax

NAUX = 2560
NVIRT = 8000
NOCC = 4


def draw_three_center(key, part):
    key_factors, key_basis, key_noise = jax.random.split(key, 3)
    width = NOCC * NVIRT
    factor_count = 16
    scale = 1.5 * width ** (-0.5)
    factors = jax.random.normal(key_factors, (NAUX, factor_count), jnp.float32)
    basis = jax.random.normal(key_basis, (factor_count, width), jnp.float32)
    shared = jnp.dot(factors, basis, precision=lax.Precision.HIGHEST) * factor_count ** (-0.5)
    noise = jax.random.normal(key_noise, (NAUX, width), jnp.float32)
    mixed = 0.5 * noise + 0.866 * shared
    mixed = jnp.clip(mixed, -6.0, 6.0)
    return (scale * mixed).reshape(NAUX, NOCC, NVIRT).astype(jnp.bfloat16)


def levels(own_key, dims, pieces, smallest, top_value):
    loudness, own = 1.0, jax.random.fold_in(own_key, 6)
    for position, blocks in pieces:
        steps = jnp.exp(jax.random.uniform(jax.random.fold_in(own, position), (blocks,), jnp.float32, smallest / len(pieces), top_value / len(pieces)))
        loudness = loudness * jnp.repeat(steps, dims[position] // blocks).reshape([-1 if axis == position else 1 for axis in range(len(dims))])
    return loudness


def setup_inputs(seed: int = 0, part: int = 0) -> dict:
    key_of = jax.random.split(jax.random.key(seed), 5)
    part_keys = jax.random.split(jax.random.fold_in(key_of[4], part), 5)
    three_center = draw_three_center(jax.random.fold_in(jax.random.fold_in(key_of[4], part), 71), part)
    eps_occ = jnp.clip(jax.random.uniform(part_keys[1], (NOCC,), jnp.float32, -1.2, -0.4), -1.2, -0.4)
    eps_virt = jnp.clip(0.2 + 2.8 * jax.random.uniform(part_keys[2], (NVIRT,), jnp.float32) ** levels(part_keys[2], (NVIRT,), ((0, 4),), -0.2, 0.2), 0.2, 3.0)
    freq = jnp.clip(jnp.exp(jax.random.uniform(part_keys[3], (1,), jnp.float32, math.log(0.2), math.log(2.0))), 0.2, 2.0)
    return dict(three_center=three_center, eps_occ=eps_occ, eps_virt=eps_virt, freq=freq)


def reference(three_center, eps_occ, eps_virt, freq):
    excite = eps_virt[None, :] - eps_occ[:, None]
    weight = 2.0 * excite / (excite * excite + freq[0] * freq[0])
    scaled = (three_center.astype(jnp.float32) * weight[None, :, :]).astype(jnp.bfloat16)
    left = scaled.reshape(NAUX, NOCC * NVIRT)
    right = three_center.reshape(NAUX, NOCC * NVIRT)
    blocks = left.reshape(8, NAUX // 8, NOCC * NVIRT)

    def one_block(rows):
        return lax.dot_general(rows, right, (((1,), (1,)), ((), ())), preferred_element_type=jnp.float32)

    return lax.map(one_block, blocks).reshape(NAUX, NAUX)
```

```python
import functools
import jax
import jax.numpy as jnp
from jax import lax
from jax.experimental import pallas as pl
from jax.experimental.pallas import tpu as pltpu
from jax.sharding import PartitionSpec as P

MESH = pl.DeviceIdType.MESH


def gather_kernel(sizes, x_ref, g_ref, zs, zr, xs, xr, cs, cr, ls):
    n_pair, n_aux, n_rep, chunks, rows = sizes
    z = lax.axis_index("pair")
    a = lax.axis_index("aux")
    r = lax.axis_index("rep")
    step = rows // chunks

    def turn(i, k, n):
        return lax.rem(i + k, n)

    peers = (
        [("pair", turn(z, k, n_pair)) for k in range(1, n_pair)]
        + [("aux", turn(a, k, n_aux)) for k in range(1, n_aux)]
        + [("rep", turn(r, k, n_rep)) for k in range(1, n_rep)]
    )
    barrier = pltpu.get_barrier_semaphore()
    for name, index in peers:
        pl.semaphore_signal(barrier, inc=1, device_id={name: index}, device_id_type=MESH)
    pl.semaphore_wait(barrier, len(peers))

    def block(aux, rep, pair, c):
        return g_ref.at[aux, rep, pair, pl.ds(c * step, step)]

    def z_copy(c, k, sending):
        to = turn(z, k, n_pair)
        src = turn(z, n_pair - k, n_pair)
        return pltpu.make_async_remote_copy(
            src_ref=x_ref.at[to, pl.ds(c * step, step)],
            dst_ref=block(a, r, z if sending else src, c),
            send_sem=zs.at[c, k],
            recv_sem=zr.at[c, k],
            device_id={"pair": to},
            device_id_type=MESH,
        )

    def x_copy(c, k, j, sending):
        pair = turn(z, n_pair - j, n_pair)
        mine = a if sending else turn(a, n_aux - k, n_aux)
        if j == 0 and sending:
            src = x_ref.at[z, pl.ds(c * step, step)]
        else:
            src = block(mine, r, pair, c)
        return pltpu.make_async_remote_copy(
            src_ref=src,
            dst_ref=block(mine, r, pair, c),
            send_sem=xs.at[c, k, j],
            recv_sem=xr.at[c, k, j],
            device_id={"aux": turn(a, k, n_aux)},
            device_id_type=MESH,
        )

    def c_copy(c, m, k, j, sending):
        pair = turn(z, n_pair - j, n_pair)
        aux = turn(a, n_aux - k, n_aux)
        rep = r if sending else turn(r, n_rep - m, n_rep)
        if j == 0 and k == 0 and sending:
            src = x_ref.at[z, pl.ds(c * step, step)]
        else:
            src = block(aux, rep, pair, c)
        return pltpu.make_async_remote_copy(
            src_ref=src,
            dst_ref=block(aux, rep, pair, c),
            send_sem=cs.at[c, m, k, j],
            recv_sem=cr.at[c, m, k, j],
            device_id={"rep": turn(r, m, n_rep)},
            device_id_type=MESH,
        )

    for c in range(chunks):
        for k in range(1, n_pair):
            z_copy(c, k, True).start()
    own = pltpu.make_async_copy(x_ref.at[z], g_ref.at[a, r, z], ls)
    own.start()

    def arrived(c, j):
        if j:
            z_copy(c, j, False).wait_recv()
        for k in range(1, n_aux):
            x_copy(c, k, j, True).start()
        for m in range(1, n_rep):
            c_copy(c, m, 0, j, True).start()

    def crossed(c, j):
        for k in range(1, n_aux):
            x_copy(c, k, j, False).wait_recv()
            for m in range(1, n_rep):
                c_copy(c, m, k, j, True).start()

    for c in range(chunks):
        arrived(c, 0)
    for c in range(chunks):
        for j in range(1, n_pair):
            arrived(c, j)
        crossed(c, 0)
        if c:
            for j in range(1, n_pair):
                crossed(c - 1, j)
    for j in range(1, n_pair):
        crossed(chunks - 1, j)

    own.wait()
    for c in range(chunks):
        for k in range(1, n_pair):
            z_copy(c, k, True).wait_send()
        for j in range(n_pair):
            for k in range(1, n_aux):
                x_copy(c, k, j, True).wait_send()
            for m in range(1, n_rep):
                for k in range(n_aux):
                    c_copy(c, m, k, j, True).wait_send()
                    c_copy(c, m, k, j, False).wait_recv()


def gather(pieces, n_aux, n_rep):
    n_pair, rows, width = pieces.shape
    chunks = 5 if rows % 80 == 0 else 1
    sizes = (n_pair, n_aux, n_rep, chunks, rows)
    dma = pltpu.SemaphoreType.DMA
    return pl.pallas_call(
        functools.partial(gather_kernel, sizes),
        out_shape=jax.ShapeDtypeStruct((n_aux, n_rep, n_pair, rows, width), pieces.dtype),
        in_specs=[pl.BlockSpec(memory_space=pl.ANY)],
        out_specs=pl.BlockSpec(memory_space=pl.ANY),
        scratch_shapes=[
            dma((chunks, n_pair)),
            dma((chunks, n_pair)),
            dma((chunks, n_aux, n_pair)),
            dma((chunks, n_aux, n_pair)),
            dma((chunks, n_rep, n_aux, n_pair)),
            dma((chunks, n_rep, n_aux, n_pair)),
            dma,
        ],
        compiler_params=pltpu.CompilerParams(collective_id=0, has_side_effects=True),
    )(pieces)


def local(mesh, three_center, eps_occ, eps_virt, freq):
    n_pair, n_aux, n_rep = (mesh.shape[name] for name in ("pair", "aux", "rep"))
    rows, n_occ, n_virt = three_center.shape
    parts = n_pair // n_occ
    width = n_virt // parts
    every_virt = lax.all_gather(eps_virt, "pair", axis=0, tiled=True)
    pieces = three_center.reshape(rows, n_pair, width).transpose(1, 0, 2)
    gathered = gather(pieces, n_aux, n_rep)

    z = lax.axis_index("pair")
    virt = lax.dynamic_slice_in_dim(every_virt, lax.rem(z, parts) * width, width)
    occ = lax.dynamic_index_in_dim(eps_occ, z // parts, keepdims=False)
    excite = virt - occ
    weight = 2.0 * excite / (excite * excite + freq[0] * freq[0])
    plain = gathered.reshape(n_aux * n_rep, n_pair * rows, width)
    mine = lax.axis_index("aux") * n_rep + lax.axis_index("rep")
    own = lax.dynamic_index_in_dim(plain, mine, keepdims=False)
    scaled = (own.astype(jnp.float32) * weight[None, :]).astype(jnp.bfloat16)
    partial_sums = lax.dot_general(
        scaled,
        plain.reshape(-1, width),
        (((1,), (1,)), ((), ())),
        preferred_element_type=jnp.float32,
    )
    return lax.psum_scatter(partial_sums, "pair", scatter_dimension=1, tiled=True)


def solution(mesh):
    return jax.shard_map(
        functools.partial(local, mesh),
        mesh=mesh,
        in_specs=(
            P(("grp", "aux", "rep", "pair"), None, None),
            P("grp"),
            P(("grp", "pair")),
            P("grp"),
        ),
        out_specs=P(("grp", "aux", "rep"), "pair"),
        check_vma=False,
    )
```

```python
import functools
import jax
import jax.numpy as jnp
from jax import lax
from jax.experimental import pallas as pl
from jax.experimental.pallas import tpu as pltpu
from jax.sharding import PartitionSpec as P

MESH = pl.DeviceIdType.MESH


def gather_kernel(sizes, x_ref, g_ref, zs, zr, xs, xr, cs, cr, ls):
    n_pair, n_aux, n_rep, chunks, rows = sizes
    z = lax.axis_index("pair")
    a = lax.axis_index("aux")
    r = lax.axis_index("rep")
    step = rows // chunks

    def turn(i, k, n):
        return lax.rem(i + k, n)

    peers = (
        [("pair", turn(z, k, n_pair)) for k in range(1, n_pair)]
        + [("aux", turn(a, k, n_aux)) for k in range(1, n_aux)]
        + [("rep", turn(r, k, n_rep)) for k in range(1, n_rep)]
    )
    barrier = pltpu.get_barrier_semaphore()
    for name, index in peers:
        pl.semaphore_signal(barrier, inc=1, device_id={name: index}, device_id_type=MESH)
    pl.semaphore_wait(barrier, len(peers))

    def block(aux, rep, pair, c):
        return g_ref.at[aux, rep, pair, pl.ds(c * step, step)]

    def z_copy(c, k, sending):
        to = turn(z, k, n_pair)
        src = turn(z, n_pair - k, n_pair)
        return pltpu.make_async_remote_copy(
            src_ref=x_ref.at[to, pl.ds(c * step, step)],
            dst_ref=block(a, r, z if sending else src, c),
            send_sem=zs.at[c, k],
            recv_sem=zr.at[c, k],
            device_id={"pair": to},
            device_id_type=MESH,
        )

    def x_copy(c, k, j, sending):
        pair = turn(z, n_pair - j, n_pair)
        mine = a if sending else turn(a, n_aux - k, n_aux)
        if j == 0 and sending:
            src = x_ref.at[z, pl.ds(c * step, step)]
        else:
            src = block(mine, r, pair, c)
        return pltpu.make_async_remote_copy(
            src_ref=src,
            dst_ref=block(mine, r, pair, c),
            send_sem=xs.at[c, k, j],
            recv_sem=xr.at[c, k, j],
            device_id={"aux": turn(a, k, n_aux)},
            device_id_type=MESH,
        )

    def c_copy(c, m, k, j, sending):
        pair = turn(z, n_pair - j, n_pair)
        aux = turn(a, n_aux - k, n_aux)
        rep = r if sending else turn(r, n_rep - m, n_rep)
        if j == 0 and k == 0 and sending:
            src = x_ref.at[z, pl.ds(c * step, step)]
        else:
            src = block(aux, rep, pair, c)
        return pltpu.make_async_remote_copy(
            src_ref=src,
            dst_ref=block(aux, rep, pair, c),
            send_sem=cs.at[c, m, k, j],
            recv_sem=cr.at[c, m, k, j],
            device_id={"rep": turn(r, m, n_rep)},
            device_id_type=MESH,
        )

    for c in range(chunks):
        for k in range(1, n_pair):
            z_copy(c, k, True).start()
    own = pltpu.make_async_copy(x_ref.at[z], g_ref.at[a, r, z], ls)
    own.start()

    def arrived(c, j):
        if j:
            z_copy(c, j, False).wait_recv()
        for k in range(1, n_aux):
            x_copy(c, k, j, True).start()
        for m in range(1, n_rep):
            c_copy(c, m, 0, j, True).start()

    def crossed(c, j):
        for k in range(1, n_aux):
            x_copy(c, k, j, False).wait_recv()
            for m in range(1, n_rep):
                c_copy(c, m, k, j, True).start()

    for c in range(chunks):
        arrived(c, 0)
    for c in range(chunks):
        for j in range(1, n_pair):
            arrived(c, j)
        crossed(c, 0)
        if c:
            for j in range(1, n_pair):
                crossed(c - 1, j)
    for j in range(1, n_pair):
        crossed(chunks - 1, j)

    own.wait()
    for c in range(chunks):
        for k in range(1, n_pair):
            z_copy(c, k, True).wait_send()
        for j in range(n_pair):
            for k in range(1, n_aux):
                x_copy(c, k, j, True).wait_send()
            for m in range(1, n_rep):
                for k in range(n_aux):
                    c_copy(c, m, k, j, True).wait_send()
                    c_copy(c, m, k, j, False).wait_recv()


def gather(pieces, n_aux, n_rep):
    n_pair, rows, width = pieces.shape
    chunks = 5 if rows % 80 == 0 else 1
    sizes = (n_pair, n_aux, n_rep, chunks, rows)
    dma = pltpu.SemaphoreType.DMA
    return pl.pallas_call(
        functools.partial(gather_kernel, sizes),
        out_shape=jax.ShapeDtypeStruct((n_aux, n_rep, n_pair, rows, width), pieces.dtype),
        in_specs=[pl.BlockSpec(memory_space=pl.ANY)],
        out_specs=pl.BlockSpec(memory_space=pl.ANY),
        scratch_shapes=[
            dma((chunks, n_pair)),
            dma((chunks, n_pair)),
            dma((chunks, n_aux, n_pair)),
            dma((chunks, n_aux, n_pair)),
            dma((chunks, n_rep, n_aux, n_pair)),
            dma((chunks, n_rep, n_aux, n_pair)),
            dma,
        ],
        compiler_params=pltpu.CompilerParams(collective_id=0, has_side_effects=True),
    )(pieces)


def fused_kernel(sizes, x_ref, w_ref, o_ref, g, p, s1, s2, lhs, zs, zr, xs, xr, cs, cr, ls, s1s, s1r, s2s, s2r):
    n_pair, n_aux, n_rep, chunks, step, width = sizes
    z = lax.axis_index("pair")
    a = lax.axis_index("aux")
    r = lax.axis_index("rep")
    mine = a * n_rep + r
    tall = n_pair * step

    def turn(i, k, n):
        return lax.rem(i + k, n)

    peers = (
        [("pair", turn(z, k, n_pair)) for k in range(1, n_pair)]
        + [("aux", turn(a, k, n_aux)) for k in range(1, n_aux)]
        + [("rep", turn(r, k, n_rep)) for k in range(1, n_rep)]
    )
    barrier = pltpu.get_barrier_semaphore()
    for name, index in peers:
        pl.semaphore_signal(barrier, inc=1, device_id={name: index}, device_id_type=MESH)
    pl.semaphore_wait(barrier, len(peers))

    def send(src, dst, send_sem, recv_sem, name, to):
        return pltpu.make_async_remote_copy(
            src_ref=src,
            dst_ref=dst,
            send_sem=send_sem,
            recv_sem=recv_sem,
            device_id={name: to},
            device_id_type=MESH,
        )

    def z_copy(c, k, sending):
        to = turn(z, k, n_pair)
        pair = z if sending else turn(z, n_pair - k, n_pair)
        return send(x_ref.at[to, c], g.at[c, mine, pair], zs.at[c, k], zr.at[c, k], "pair", to)

    def x_copy(c, k, j, sending):
        pair = turn(z, n_pair - j, n_pair)
        aux = a if sending else turn(a, n_aux - k, n_aux)
        dst = g.at[c, aux * n_rep + r, pair]
        src = x_ref.at[z, c] if j == 0 and sending else dst
        return send(src, dst, xs.at[c, k, j], xr.at[c, k, j], "aux", turn(a, k, n_aux))

    def c_copy(c, m, k, j, sending):
        pair = turn(z, n_pair - j, n_pair)
        aux = turn(a, n_aux - k, n_aux)
        rep = r if sending else turn(r, n_rep - m, n_rep)
        dst = g.at[c, aux * n_rep + rep, pair]
        src = x_ref.at[z, c] if j == 0 and k == 0 and sending else dst
        return send(src, dst, cs.at[c, m, k, j], cr.at[c, m, k, j], "rep", turn(r, m, n_rep))

    def start_z(c):
        if c < chunks:
            for k in range(1, n_pair):
                z_copy(c, k, True).start()

    def arrived(c, j):
        if j:
            z_copy(c, j, False).wait_recv()
        for k in range(1, n_aux):
            x_copy(c, k, j, True).start()
        for m in range(1, n_rep):
            c_copy(c, m, 0, j, True).start()

    def crossed(c, j):
        for k in range(1, n_aux):
            x_copy(c, k, j, False).wait_recv()
            for m in range(1, n_rep):
                c_copy(c, m, k, j, True).start()

    def complete(c):
        for j in range(n_pair):
            for m in range(1, n_rep):
                for k in range(n_aux):
                    c_copy(c, m, k, j, False).wait_recv()

    odd = lax.rem(z, 2)
    near = z + 1 - 2 * odd
    far = lax.rem(z + 2, 4)
    half = lax.div(z, 2)

    def span(c):
        return pl.ds(c * c, 2 * c + 1)

    def first(c, b):
        block = 1 - odd + 2 * b
        return send(p.at[block, span(c)], s1.at[b, span(c)], s1s.at[c, b], s1r.at[c, b], "pair", near)

    def second(c):
        return send(p.at[far, span(c)], s2.at[span(c)], s2s.at[c], s2r.at[c], "pair", far)

    def scale(c):
        own = g[c, mine].reshape(tall, width).astype(jnp.float32)
        lhs[...] = (own * w_ref[...]).astype(jnp.bfloat16)

    def tiles(c, t):
        @pl.loop(0, n_aux * n_rep // 2)
        def _(h):
            rhs = g[c, pl.ds(2 * h, 2)].reshape(2 * tall, width)
            got = lax.dot_general(
                lhs[...], rhs, (((1,), (1,)), ((), ())), preferred_element_type=jnp.float32
            )
            p[2 * h, t] = got[:, :tall]
            p[2 * h + 1, t] = got[:, tall:]

    def compute(c):
        if c:
            @pl.loop(0, c)
            def _(i):
                scale(i)
                tiles(c, c * c + i)

        scale(c)

        @pl.loop(0, c + 1)
        def _(i):
            tiles(i, c * c + c + i)

        for b in range(2):
            first(c, b).start()

    def halve(c):
        for b in range(2):
            first(c, b).wait_recv()

        @pl.loop(c * c, (c + 1) * (c + 1))
        def _(t):
            p[far, t] += s1[1 - half, t]

        second(c).start()

        @pl.loop(c * c, (c + 1) * (c + 1))
        def _(t):
            p[z, t] += s1[half, t]

    def finish(c):
        second(c).wait_recv()
        if c:
            @pl.loop(0, c)
            def _(i):
                o_ref[i, c] = p[z, c * c + i] + s2[c * c + i]

        @pl.loop(0, c + 1)
        def _(i):
            o_ref[c, i] = p[z, c * c + c + i] + s2[c * c + c + i]

    start_z(0)
    start_z(1)
    own = pltpu.make_async_copy(x_ref.at[z], g.at[:, mine, z], ls)
    own.start()
    for c in range(chunks):
        arrived(c, 0)
    own.wait()
    for c in range(chunks + 1):
        if c < chunks:
            for j in range(1, n_pair):
                arrived(c, j)
            start_z(c + 2)
        if c:
            for j in range(n_pair):
                crossed(c - 1, j)
            complete(c - 1)
            compute(c - 1)
        if c > 1:
            halve(c - 2)
        if c > 2:
            finish(c - 3)
    halve(chunks - 1)
    finish(chunks - 2)
    finish(chunks - 1)

    for c in range(chunks):
        second(c).wait_send()
        for b in range(2):
            first(c, b).wait_send()
        for k in range(1, n_pair):
            z_copy(c, k, True).wait_send()
        for j in range(n_pair):
            for k in range(1, n_aux):
                x_copy(c, k, j, True).wait_send()
            for m in range(1, n_rep):
                for k in range(n_aux):
                    c_copy(c, m, k, j, True).wait_send()


def fused(pieces, weight, n_aux, n_rep):
    n_pair, chunks, step, width = pieces.shape
    tall = n_pair * step
    groups = n_aux * n_rep
    sizes = (n_pair, n_aux, n_rep, chunks, step, width)
    dma = pltpu.SemaphoreType.DMA
    return pl.pallas_call(
        functools.partial(fused_kernel, sizes),
        out_shape=jax.ShapeDtypeStruct((chunks, chunks, tall, tall), jnp.float32),
        in_specs=[pl.BlockSpec(memory_space=pl.ANY), pl.BlockSpec(memory_space=pltpu.VMEM)],
        out_specs=pl.BlockSpec(memory_space=pltpu.VMEM),
        scratch_shapes=[
            pltpu.VMEM((chunks, groups, n_pair, step, width), jnp.bfloat16),
            pltpu.VMEM((groups, chunks * chunks, tall, tall), jnp.float32),
            pltpu.VMEM((2, chunks * chunks, tall, tall), jnp.float32),
            pltpu.VMEM((chunks * chunks, tall, tall), jnp.float32),
            pltpu.VMEM((tall, width), jnp.bfloat16),
            dma((chunks, n_pair)),
            dma((chunks, n_pair)),
            dma((chunks, n_aux, n_pair)),
            dma((chunks, n_aux, n_pair)),
            dma((chunks, n_rep, n_aux, n_pair)),
            dma((chunks, n_rep, n_aux, n_pair)),
            dma,
            dma((chunks, 2)),
            dma((chunks, 2)),
            dma((chunks,)),
            dma((chunks,)),
        ],
        compiler_params=pltpu.CompilerParams(
            collective_id=1, has_side_effects=True, vmem_limit_bytes=60 * 2**20
        ),
    )(pieces, weight)


def local(mesh, three_center, eps_occ, eps_virt, freq):
    n_pair, n_aux, n_rep = (mesh.shape[name] for name in ("pair", "aux", "rep"))
    rows, n_occ, n_virt = three_center.shape
    if n_pair == n_occ == n_aux * n_rep == 4 and rows % 32 == 0:
        return whole_kernel(n_aux, n_rep, three_center, eps_occ, eps_virt, freq)
    return staged(n_pair, n_aux, n_rep, three_center, eps_occ, eps_virt, freq)


def whole_kernel(n_aux, n_rep, three_center, eps_occ, eps_virt, freq):
    rows, n_pair, n_virt = three_center.shape
    pad = -n_virt % 128
    chunks = rows // 32
    virt = lax.all_gather(eps_virt, "pair", axis=0, tiled=True)
    occ = lax.dynamic_index_in_dim(eps_occ, lax.axis_index("pair"), keepdims=False)
    excite = virt - occ
    weight = 2.0 * excite / (excite * excite + freq[0] * freq[0])
    weight = jnp.pad(weight, (0, pad))[None, :]
    pieces = jnp.pad(three_center.transpose(1, 0, 2), ((0, 0), (0, 0), (0, pad)))
    pieces = pieces.reshape(n_pair, chunks, 32, n_virt + pad)
    out = fused(pieces, weight, n_aux, n_rep)
    out = out.reshape(chunks, chunks, n_pair, 32, n_pair, 32)
    return out.transpose(2, 0, 3, 4, 1, 5).reshape(n_pair * rows, n_pair * rows)


def staged(n_pair, n_aux, n_rep, three_center, eps_occ, eps_virt, freq):
    rows, n_occ, n_virt = three_center.shape
    parts = n_pair // n_occ
    width = n_virt // parts
    every_virt = lax.all_gather(eps_virt, "pair", axis=0, tiled=True)
    pieces = three_center.reshape(rows, n_pair, width).transpose(1, 0, 2)
    gathered = gather(pieces, n_aux, n_rep)

    z = lax.axis_index("pair")
    virt = lax.dynamic_slice_in_dim(every_virt, lax.rem(z, parts) * width, width)
    occ = lax.dynamic_index_in_dim(eps_occ, z // parts, keepdims=False)
    excite = virt - occ
    weight = 2.0 * excite / (excite * excite + freq[0] * freq[0])
    plain = gathered.reshape(n_aux * n_rep, n_pair * rows, width)
    mine = lax.axis_index("aux") * n_rep + lax.axis_index("rep")
    own = lax.dynamic_index_in_dim(plain, mine, keepdims=False)
    scaled = (own.astype(jnp.float32) * weight[None, :]).astype(jnp.bfloat16)
    partial_sums = lax.dot_general(
        scaled,
        plain.reshape(-1, width),
        (((1,), (1,)), ((), ())),
        preferred_element_type=jnp.float32,
    )
    return lax.psum_scatter(partial_sums, "pair", scatter_dimension=1, tiled=True)


def solution(mesh):
    return jax.shard_map(
        functools.partial(local, mesh),
        mesh=mesh,
        in_specs=(
            P(("grp", "aux", "rep", "pair"), None, None),
            P("grp"),
            P(("grp", "pair")),
            P("grp"),
        ),
        out_specs=P(("grp", "aux", "rep"), "pair"),
        check_vma=False,
    )
```

```python
import functools
import jax
import jax.numpy as jnp
from jax import lax
from jax.experimental import pallas as pl
from jax.experimental.pallas import tpu as pltpu
from jax.sharding import PartitionSpec as P

MESH = pl.DeviceIdType.MESH


def gather_kernel(sizes, x_ref, g_ref, zs, zr, xs, xr, cs, cr, ls):
    n_pair, n_aux, n_rep, chunks, rows = sizes
    z = lax.axis_index("pair")
    a = lax.axis_index("aux")
    r = lax.axis_index("rep")
    step = rows // chunks

    def turn(i, k, n):
        return lax.rem(i + k, n)

    peers = (
        [("pair", turn(z, k, n_pair)) for k in range(1, n_pair)]
        + [("aux", turn(a, k, n_aux)) for k in range(1, n_aux)]
        + [("rep", turn(r, k, n_rep)) for k in range(1, n_rep)]
    )
    barrier = pltpu.get_barrier_semaphore()
    for name, index in peers:
        pl.semaphore_signal(barrier, inc=1, device_id={name: index}, device_id_type=MESH)
    pl.semaphore_wait(barrier, len(peers))

    def block(aux, rep, pair, c):
        return g_ref.at[aux, rep, pair, pl.ds(c * step, step)]

    def z_copy(c, k, sending):
        to = turn(z, k, n_pair)
        src = turn(z, n_pair - k, n_pair)
        return pltpu.make_async_remote_copy(
            src_ref=x_ref.at[to, pl.ds(c * step, step)],
            dst_ref=block(a, r, z if sending else src, c),
            send_sem=zs.at[c, k],
            recv_sem=zr.at[c, k],
            device_id={"pair": to},
            device_id_type=MESH,
        )

    def x_copy(c, k, j, sending):
        pair = turn(z, n_pair - j, n_pair)
        mine = a if sending else turn(a, n_aux - k, n_aux)
        if j == 0 and sending:
            src = x_ref.at[z, pl.ds(c * step, step)]
        else:
            src = block(mine, r, pair, c)
        return pltpu.make_async_remote_copy(
            src_ref=src,
            dst_ref=block(mine, r, pair, c),
            send_sem=xs.at[c, k, j],
            recv_sem=xr.at[c, k, j],
            device_id={"aux": turn(a, k, n_aux)},
            device_id_type=MESH,
        )

    def c_copy(c, m, k, j, sending):
        pair = turn(z, n_pair - j, n_pair)
        aux = turn(a, n_aux - k, n_aux)
        rep = r if sending else turn(r, n_rep - m, n_rep)
        if j == 0 and k == 0 and sending:
            src = x_ref.at[z, pl.ds(c * step, step)]
        else:
            src = block(aux, rep, pair, c)
        return pltpu.make_async_remote_copy(
            src_ref=src,
            dst_ref=block(aux, rep, pair, c),
            send_sem=cs.at[c, m, k, j],
            recv_sem=cr.at[c, m, k, j],
            device_id={"rep": turn(r, m, n_rep)},
            device_id_type=MESH,
        )

    for c in range(chunks):
        for k in range(1, n_pair):
            z_copy(c, k, True).start()
    own = pltpu.make_async_copy(x_ref.at[z], g_ref.at[a, r, z], ls)
    own.start()

    def arrived(c, j):
        if j:
            z_copy(c, j, False).wait_recv()
        for k in range(1, n_aux):
            x_copy(c, k, j, True).start()
        for m in range(1, n_rep):
            c_copy(c, m, 0, j, True).start()

    def crossed(c, j):
        for k in range(1, n_aux):
            x_copy(c, k, j, False).wait_recv()
            for m in range(1, n_rep):
                c_copy(c, m, k, j, True).start()

    for c in range(chunks):
        arrived(c, 0)
    for c in range(chunks):
        for j in range(1, n_pair):
            arrived(c, j)
        crossed(c, 0)
        if c:
            for j in range(1, n_pair):
                crossed(c - 1, j)
    for j in range(1, n_pair):
        crossed(chunks - 1, j)

    own.wait()
    for c in range(chunks):
        for k in range(1, n_pair):
            z_copy(c, k, True).wait_send()
        for j in range(n_pair):
            for k in range(1, n_aux):
                x_copy(c, k, j, True).wait_send()
            for m in range(1, n_rep):
                for k in range(n_aux):
                    c_copy(c, m, k, j, True).wait_send()
                    c_copy(c, m, k, j, False).wait_recv()


def gather(pieces, n_aux, n_rep):
    n_pair, rows, width = pieces.shape
    chunks = 5 if rows % 80 == 0 else 1
    sizes = (n_pair, n_aux, n_rep, chunks, rows)
    dma = pltpu.SemaphoreType.DMA
    return pl.pallas_call(
        functools.partial(gather_kernel, sizes),
        out_shape=jax.ShapeDtypeStruct((n_aux, n_rep, n_pair, rows, width), pieces.dtype),
        in_specs=[pl.BlockSpec(memory_space=pl.ANY)],
        out_specs=pl.BlockSpec(memory_space=pl.ANY),
        scratch_shapes=[
            dma((chunks, n_pair)),
            dma((chunks, n_pair)),
            dma((chunks, n_aux, n_pair)),
            dma((chunks, n_aux, n_pair)),
            dma((chunks, n_rep, n_aux, n_pair)),
            dma((chunks, n_rep, n_aux, n_pair)),
            dma,
        ],
        compiler_params=pltpu.CompilerParams(collective_id=0, has_side_effects=True),
    )(pieces)


def fused_kernel(
    sizes, x_ref, occ_ref, virt_ref, freq_ref, o_ref, g, p, s1, s2, lhs, levels, w_ref,
    zs, zr, xs, xr, cs, cr, ls, s1s, s1r, s2s, s2r, es, er,
):
    n_pair, n_aux, n_rep, chunks, step, width = sizes
    z = lax.axis_index("pair")
    a = lax.axis_index("aux")
    r = lax.axis_index("rep")
    mine = a * n_rep + r
    tall = n_pair * step

    def turn(i, k, n):
        return lax.rem(i + k, n)

    peers = (
        [("pair", turn(z, k, n_pair)) for k in range(1, n_pair)]
        + [("aux", turn(a, k, n_aux)) for k in range(1, n_aux)]
        + [("rep", turn(r, k, n_rep)) for k in range(1, n_rep)]
    )
    barrier = pltpu.get_barrier_semaphore()
    for name, index in peers:
        pl.semaphore_signal(barrier, inc=1, device_id={name: index}, device_id_type=MESH)
    pl.semaphore_wait(barrier, len(peers))

    def send(src, dst, send_sem, recv_sem, name, to):
        return pltpu.make_async_remote_copy(
            src_ref=src,
            dst_ref=dst,
            send_sem=send_sem,
            recv_sem=recv_sem,
            device_id={name: to},
            device_id_type=MESH,
        )

    def z_copy(c, k, sending):
        to = turn(z, k, n_pair)
        pair = z if sending else turn(z, n_pair - k, n_pair)
        return send(x_ref.at[to, c], g.at[c, mine, pair], zs.at[c, k], zr.at[c, k], "pair", to)

    def x_copy(c, k, j, sending):
        pair = turn(z, n_pair - j, n_pair)
        aux = a if sending else turn(a, n_aux - k, n_aux)
        dst = g.at[c, aux * n_rep + r, pair]
        src = x_ref.at[z, c] if j == 0 and sending else dst
        return send(src, dst, xs.at[c, k, j], xr.at[c, k, j], "aux", turn(a, k, n_aux))

    def c_copy(c, m, k, j, sending):
        pair = turn(z, n_pair - j, n_pair)
        aux = turn(a, n_aux - k, n_aux)
        rep = r if sending else turn(r, n_rep - m, n_rep)
        dst = g.at[c, aux * n_rep + rep, pair]
        src = x_ref.at[z, c] if j == 0 and k == 0 and sending else dst
        return send(src, dst, cs.at[c, m, k, j], cr.at[c, m, k, j], "rep", turn(r, m, n_rep))

    def start_z(c):
        if c < chunks:
            for k in range(1, n_pair):
                z_copy(c, k, True).start()

    def arrived(c, j):
        if j:
            z_copy(c, j, False).wait_recv()
        for k in range(1, n_aux):
            x_copy(c, k, j, True).start()
        for m in range(1, n_rep):
            c_copy(c, m, 0, j, True).start()

    def crossed(c, j):
        for k in range(1, n_aux):
            x_copy(c, k, j, False).wait_recv()
            for m in range(1, n_rep):
                c_copy(c, m, k, j, True).start()

    def complete(c):
        for j in range(n_pair):
            for m in range(1, n_rep):
                for k in range(n_aux):
                    c_copy(c, m, k, j, False).wait_recv()

    odd = lax.rem(z, 2)
    near = z + 1 - 2 * odd
    far = lax.rem(z + 2, 4)
    half = lax.div(z, 2)

    def span(c):
        return pl.ds(c * c, 2 * c + 1)

    def first(c, b):
        block = 1 - odd + 2 * b
        return send(p.at[block, span(c)], s1.at[b, span(c)], s1s.at[c, b], s1r.at[c, b], "pair", near)

    def second(c):
        return send(p.at[far, span(c)], s2.at[span(c)], s2s.at[c], s2r.at[c], "pair", far)

    def e_copy(k, sending):
        pair = z if sending else turn(z, n_pair - k, n_pair)
        return send(virt_ref, levels.at[pair], es.at[k], er.at[k], "pair", turn(z, k, n_pair))

    def weigh():
        levels[z] = virt_ref[...]
        for k in range(1, n_pair):
            e_copy(k, False).wait_recv()
        freq = freq_ref[0]
        piece = virt_ref.shape[1]
        for k in range(n_pair):
            excite = levels[k] - occ_ref[z]
            w_ref[:, k * piece : (k + 1) * piece] = 2.0 * excite / (excite * excite + freq * freq)

    def scale(c):
        own = g[c, mine].reshape(tall, width).astype(jnp.float32)
        lhs[...] = (own * w_ref[...]).astype(jnp.bfloat16)

    def tiles(c, t):
        @pl.loop(0, n_aux * n_rep // 2)
        def _(h):
            rhs = g[c, pl.ds(2 * h, 2)].reshape(2 * tall, width)
            got = lax.dot_general(
                lhs[...], rhs, (((1,), (1,)), ((), ())), preferred_element_type=jnp.float32
            )
            p[2 * h, t] = got[:, :tall]
            p[2 * h + 1, t] = got[:, tall:]

    def compute(c):
        if c:
            @pl.loop(0, c)
            def _(i):
                scale(i)
                tiles(c, c * c + i)

        scale(c)

        @pl.loop(0, c + 1)
        def _(i):
            tiles(i, c * c + c + i)

        for b in range(2):
            first(c, b).start()

    def halve(c):
        for b in range(2):
            first(c, b).wait_recv()

        @pl.loop(c * c, (c + 1) * (c + 1))
        def _(t):
            p[far, t] += s1[1 - half, t]

        second(c).start()

        @pl.loop(c * c, (c + 1) * (c + 1))
        def _(t):
            p[z, t] += s1[half, t]

    def place(c1, c2, t):
        done = p[z, t] + s2[t]
        for i in range(n_pair):
            row = pl.multiple_of(i * chunks * step + c1 * step, step)
            for j in range(n_pair):
                column = (j * chunks + c2) * step
                o_ref[pl.ds(row, step), column : column + step] = done[
                    i * step : (i + 1) * step, j * step : (j + 1) * step
                ]

    def finish(c):
        second(c).wait_recv()
        if c:
            @pl.loop(0, c)
            def _(i):
                place(i, c, c * c + i)

        for i in range(c + 1):
            place(c, i, c * c + c + i)

    for k in range(1, n_pair):
        e_copy(k, True).start()
    start_z(0)
    start_z(1)
    own = pltpu.make_async_copy(x_ref.at[z], g.at[:, mine, z], ls)
    own.start()
    for c in range(chunks):
        arrived(c, 0)
    weigh()
    own.wait()
    for c in range(chunks + 1):
        if c < chunks:
            for j in range(1, n_pair):
                arrived(c, j)
            start_z(c + 2)
        if c:
            for j in range(n_pair):
                crossed(c - 1, j)
            complete(c - 1)
            compute(c - 1)
        if c > 1:
            halve(c - 2)
        if c > 2:
            finish(c - 3)
    halve(chunks - 1)
    finish(chunks - 2)
    finish(chunks - 1)

    for k in range(1, n_pair):
        e_copy(k, True).wait_send()
    for c in range(chunks):
        second(c).wait_send()
        for b in range(2):
            first(c, b).wait_send()
        for k in range(1, n_pair):
            z_copy(c, k, True).wait_send()
        for j in range(n_pair):
            for k in range(1, n_aux):
                x_copy(c, k, j, True).wait_send()
            for m in range(1, n_rep):
                for k in range(n_aux):
                    c_copy(c, m, k, j, True).wait_send()


def fused(pieces, eps_occ, eps_virt, freq, n_aux, n_rep):
    n_pair, chunks, step, width = pieces.shape
    tall = n_pair * step
    groups = n_aux * n_rep
    sizes = (n_pair, n_aux, n_rep, chunks, step, width)
    dma = pltpu.SemaphoreType.DMA
    return pl.pallas_call(
        functools.partial(fused_kernel, sizes),
        out_shape=jax.ShapeDtypeStruct((chunks * tall, chunks * tall), jnp.float32),
        in_specs=[
            pl.BlockSpec(memory_space=pl.ANY),
            pl.BlockSpec(memory_space=pltpu.SMEM),
            pl.BlockSpec(memory_space=pltpu.VMEM),
            pl.BlockSpec(memory_space=pltpu.SMEM),
        ],
        out_specs=pl.BlockSpec(memory_space=pltpu.VMEM),
        scratch_shapes=[
            pltpu.VMEM((chunks, groups, n_pair, step, width), jnp.bfloat16),
            pltpu.VMEM((groups, chunks * chunks, tall, tall), jnp.float32),
            pltpu.VMEM((2, chunks * chunks, tall, tall), jnp.float32),
            pltpu.VMEM((chunks * chunks, tall, tall), jnp.float32),
            pltpu.VMEM((tall, width), jnp.bfloat16),
            pltpu.VMEM((n_pair, 1, width // n_pair), jnp.float32),
            pltpu.VMEM((1, width), jnp.float32),
            dma((chunks, n_pair)),
            dma((chunks, n_pair)),
            dma((chunks, n_aux, n_pair)),
            dma((chunks, n_aux, n_pair)),
            dma((chunks, n_rep, n_aux, n_pair)),
            dma((chunks, n_rep, n_aux, n_pair)),
            dma,
            dma((chunks, 2)),
            dma((chunks, 2)),
            dma((chunks,)),
            dma((chunks,)),
            dma((n_pair,)),
            dma((n_pair,)),
        ],
        compiler_params=pltpu.CompilerParams(
            collective_id=1, has_side_effects=True, vmem_limit_bytes=60 * 2**20
        ),
    )(pieces, eps_occ, eps_virt[None, :], freq)


def local(mesh, three_center, eps_occ, eps_virt, freq):
    n_pair, n_aux, n_rep = (mesh.shape[name] for name in ("pair", "aux", "rep"))
    rows, n_occ, n_virt = three_center.shape
    if n_pair == n_occ == n_aux * n_rep == 4 and rows % 32 == 0:
        return whole_kernel(n_aux, n_rep, three_center, eps_occ, eps_virt, freq)
    return staged(n_pair, n_aux, n_rep, three_center, eps_occ, eps_virt, freq)


def whole_kernel(n_aux, n_rep, three_center, eps_occ, eps_virt, freq):
    rows, n_pair, n_virt = three_center.shape
    pieces = three_center.transpose(1, 0, 2).reshape(n_pair, rows // 32, 32, n_virt)
    return fused(pieces, eps_occ, eps_virt, freq, n_aux, n_rep)


def staged(n_pair, n_aux, n_rep, three_center, eps_occ, eps_virt, freq):
    rows, n_occ, n_virt = three_center.shape
    parts = n_pair // n_occ
    width = n_virt // parts
    every_virt = lax.all_gather(eps_virt, "pair", axis=0, tiled=True)
    pieces = three_center.reshape(rows, n_pair, width).transpose(1, 0, 2)
    gathered = gather(pieces, n_aux, n_rep)

    z = lax.axis_index("pair")
    virt = lax.dynamic_slice_in_dim(every_virt, lax.rem(z, parts) * width, width)
    occ = lax.dynamic_index_in_dim(eps_occ, z // parts, keepdims=False)
    excite = virt - occ
    weight = 2.0 * excite / (excite * excite + freq[0] * freq[0])
    plain = gathered.reshape(n_aux * n_rep, n_pair * rows, width)
    mine = lax.axis_index("aux") * n_rep + lax.axis_index("rep")
    own = lax.dynamic_index_in_dim(plain, mine, keepdims=False)
    scaled = (own.astype(jnp.float32) * weight[None, :]).astype(jnp.bfloat16)
    partial_sums = lax.dot_general(
        scaled,
        plain.reshape(-1, width),
        (((1,), (1,)), ((), ())),
        preferred_element_type=jnp.float32,
    )
    return lax.psum_scatter(partial_sums, "pair", scatter_dimension=1, tiled=True)


def solution(mesh):
    return jax.shard_map(
        functools.partial(local, mesh),
        mesh=mesh,
        in_specs=(
            P(("grp", "aux", "rep", "pair"), None, None),
            P("grp"),
            P(("grp", "pair")),
            P("grp"),
        ),
        out_specs=P(("grp", "aux", "rep"), "pair"),
        check_vma=False,
    )
```

```python
import functools
import jax
import jax.numpy as jnp
from jax import lax
from jax.experimental import pallas as pl
from jax.experimental.pallas import tpu as pltpu
from jax.sharding import PartitionSpec as P

MESH = pl.DeviceIdType.MESH


def gather_kernel(sizes, x_ref, g_ref, zs, zr, xs, xr, cs, cr, ls):
    n_pair, n_aux, n_rep, chunks, rows = sizes
    z = lax.axis_index("pair")
    a = lax.axis_index("aux")
    r = lax.axis_index("rep")
    step = rows // chunks

    def turn(i, k, n):
        return lax.rem(i + k, n)

    peers = (
        [("pair", turn(z, k, n_pair)) for k in range(1, n_pair)]
        + [("aux", turn(a, k, n_aux)) for k in range(1, n_aux)]
        + [("rep", turn(r, k, n_rep)) for k in range(1, n_rep)]
    )
    barrier = pltpu.get_barrier_semaphore()
    for name, index in peers:
        pl.semaphore_signal(barrier, inc=1, device_id={name: index}, device_id_type=MESH)
    pl.semaphore_wait(barrier, len(peers))

    def block(aux, rep, pair, c):
        return g_ref.at[aux, rep, pair, pl.ds(c * step, step)]

    def z_copy(c, k, sending):
        to = turn(z, k, n_pair)
        src = turn(z, n_pair - k, n_pair)
        return pltpu.make_async_remote_copy(
            src_ref=x_ref.at[to, pl.ds(c * step, step)],
            dst_ref=block(a, r, z if sending else src, c),
            send_sem=zs.at[c, k],
            recv_sem=zr.at[c, k],
            device_id={"pair": to},
            device_id_type=MESH,
        )

    def x_copy(c, k, j, sending):
        pair = turn(z, n_pair - j, n_pair)
        mine = a if sending else turn(a, n_aux - k, n_aux)
        if j == 0 and sending:
            src = x_ref.at[z, pl.ds(c * step, step)]
        else:
            src = block(mine, r, pair, c)
        return pltpu.make_async_remote_copy(
            src_ref=src,
            dst_ref=block(mine, r, pair, c),
            send_sem=xs.at[c, k, j],
            recv_sem=xr.at[c, k, j],
            device_id={"aux": turn(a, k, n_aux)},
            device_id_type=MESH,
        )

    def c_copy(c, m, k, j, sending):
        pair = turn(z, n_pair - j, n_pair)
        aux = turn(a, n_aux - k, n_aux)
        rep = r if sending else turn(r, n_rep - m, n_rep)
        if j == 0 and k == 0 and sending:
            src = x_ref.at[z, pl.ds(c * step, step)]
        else:
            src = block(aux, rep, pair, c)
        return pltpu.make_async_remote_copy(
            src_ref=src,
            dst_ref=block(aux, rep, pair, c),
            send_sem=cs.at[c, m, k, j],
            recv_sem=cr.at[c, m, k, j],
            device_id={"rep": turn(r, m, n_rep)},
            device_id_type=MESH,
        )

    for c in range(chunks):
        for k in range(1, n_pair):
            z_copy(c, k, True).start()
    own = pltpu.make_async_copy(x_ref.at[z], g_ref.at[a, r, z], ls)
    own.start()

    def arrived(c, j):
        if j:
            z_copy(c, j, False).wait_recv()
        for k in range(1, n_aux):
            x_copy(c, k, j, True).start()
        for m in range(1, n_rep):
            c_copy(c, m, 0, j, True).start()

    def crossed(c, j):
        for k in range(1, n_aux):
            x_copy(c, k, j, False).wait_recv()
            for m in range(1, n_rep):
                c_copy(c, m, k, j, True).start()

    for c in range(chunks):
        arrived(c, 0)
    for c in range(chunks):
        for j in range(1, n_pair):
            arrived(c, j)
        crossed(c, 0)
        if c:
            for j in range(1, n_pair):
                crossed(c - 1, j)
    for j in range(1, n_pair):
        crossed(chunks - 1, j)

    own.wait()
    for c in range(chunks):
        for k in range(1, n_pair):
            z_copy(c, k, True).wait_send()
        for j in range(n_pair):
            for k in range(1, n_aux):
                x_copy(c, k, j, True).wait_send()
            for m in range(1, n_rep):
                for k in range(n_aux):
                    c_copy(c, m, k, j, True).wait_send()
                    c_copy(c, m, k, j, False).wait_recv()


def gather(pieces, n_aux, n_rep):
    n_pair, rows, width = pieces.shape
    chunks = 5 if rows % 80 == 0 else 1
    sizes = (n_pair, n_aux, n_rep, chunks, rows)
    dma = pltpu.SemaphoreType.DMA
    return pl.pallas_call(
        functools.partial(gather_kernel, sizes),
        out_shape=jax.ShapeDtypeStruct((n_aux, n_rep, n_pair, rows, width), pieces.dtype),
        in_specs=[pl.BlockSpec(memory_space=pl.ANY)],
        out_specs=pl.BlockSpec(memory_space=pl.ANY),
        scratch_shapes=[
            dma((chunks, n_pair)),
            dma((chunks, n_pair)),
            dma((chunks, n_aux, n_pair)),
            dma((chunks, n_aux, n_pair)),
            dma((chunks, n_rep, n_aux, n_pair)),
            dma((chunks, n_rep, n_aux, n_pair)),
            dma,
        ],
        compiler_params=pltpu.CompilerParams(collective_id=0, has_side_effects=True),
    )(pieces)


def fused_kernel(
    sizes, x_ref, occ_ref, virt_ref, freq_ref, o_ref, g, p, s1, s2, lhs, levels, w_ref,
    zs, zr, xs, xr, cs, cr, ls, s1s, s1r, s2s, s2r, es, er,
):
    n_pair, n_aux, n_rep, chunks, step, width = sizes
    z = lax.axis_index("pair")
    a = lax.axis_index("aux")
    r = lax.axis_index("rep")
    mine = a * n_rep + r
    tall = n_pair * step

    def turn(i, k, n):
        return lax.rem(i + k, n)

    peers = (
        [("pair", turn(z, k, n_pair)) for k in range(1, n_pair)]
        + [("aux", turn(a, k, n_aux)) for k in range(1, n_aux)]
        + [("rep", turn(r, k, n_rep)) for k in range(1, n_rep)]
    )
    barrier = pltpu.get_barrier_semaphore()
    for name, index in peers:
        pl.semaphore_signal(barrier, inc=1, device_id={name: index}, device_id_type=MESH)
    pl.semaphore_wait(barrier, len(peers))

    def send(src, dst, send_sem, recv_sem, name, to):
        return pltpu.make_async_remote_copy(
            src_ref=src,
            dst_ref=dst,
            send_sem=send_sem,
            recv_sem=recv_sem,
            device_id={name: to},
            device_id_type=MESH,
        )

    def z_copy(c, k, sending):
        to = turn(z, k, n_pair)
        pair = z if sending else turn(z, n_pair - k, n_pair)
        return send(x_ref.at[to, c], g.at[c, mine, pair], zs.at[c, k], zr.at[c, k], "pair", to)

    def x_copy(c, k, j, sending):
        pair = turn(z, n_pair - j, n_pair)
        aux = a if sending else turn(a, n_aux - k, n_aux)
        dst = g.at[c, aux * n_rep + r, pair]
        src = x_ref.at[z, c] if j == 0 and sending else dst
        return send(src, dst, xs.at[c, k, j], xr.at[c, k, j], "aux", turn(a, k, n_aux))

    def c_copy(c, m, k, j, sending):
        pair = turn(z, n_pair - j, n_pair)
        aux = turn(a, n_aux - k, n_aux)
        rep = r if sending else turn(r, n_rep - m, n_rep)
        dst = g.at[c, aux * n_rep + rep, pair]
        src = x_ref.at[z, c] if j == 0 and k == 0 and sending else dst
        return send(src, dst, cs.at[c, m, k, j], cr.at[c, m, k, j], "rep", turn(r, m, n_rep))

    def start_z(c):
        if c < chunks:
            for k in range(1, n_pair):
                z_copy(c, k, True).start()

    def arrived(c, j):
        if j:
            z_copy(c, j, False).wait_recv()
        for k in range(1, n_aux):
            x_copy(c, k, j, True).start()
        for m in range(1, n_rep):
            c_copy(c, m, 0, j, True).start()

    def crossed(c, j):
        for k in range(1, n_aux):
            x_copy(c, k, j, False).wait_recv()
            for m in range(1, n_rep):
                c_copy(c, m, k, j, True).start()

    def complete(c):
        for j in range(n_pair):
            for m in range(1, n_rep):
                for k in range(n_aux):
                    c_copy(c, m, k, j, False).wait_recv()

    odd = lax.rem(z, 2)
    near = z + 1 - 2 * odd
    far = lax.rem(z + 2, 4)
    half = lax.div(z, 2)

    def span(c):
        return pl.ds(c * c, 2 * c + 1)

    def first(c, b):
        block = 1 - odd + 2 * b
        return send(p.at[block, span(c)], s1.at[b, span(c)], s1s.at[c, b], s1r.at[c, b], "pair", near)

    def second(c):
        return send(p.at[far, span(c)], s2.at[span(c)], s2s.at[c], s2r.at[c], "pair", far)

    def e_copy(k, sending):
        pair = z if sending else turn(z, n_pair - k, n_pair)
        return send(virt_ref, levels.at[pair], es.at[k], er.at[k], "pair", turn(z, k, n_pair))

    def weigh():
        levels[z] = virt_ref[...]
        for k in range(1, n_pair):
            e_copy(k, False).wait_recv()
        freq = freq_ref[0]
        piece = virt_ref.shape[1]
        for k in range(n_pair):
            excite = levels[k] - occ_ref[z]
            w_ref[:, k * piece : (k + 1) * piece] = 2.0 * excite / (excite * excite + freq * freq)

    def scale(c):
        own = g[c, mine].reshape(tall, width).astype(jnp.float32)
        lhs[...] = (own * w_ref[...]).astype(jnp.bfloat16)

    def tiles(c, t):
        @pl.loop(0, n_aux * n_rep // 2)
        def _(h):
            rhs = g[c, pl.ds(2 * h, 2)].reshape(2 * tall, width)
            got = lax.dot_general(
                lhs[...], rhs, (((1,), (1,)), ((), ())), preferred_element_type=jnp.float32
            )
            p[2 * h, t] = got[:, :tall]
            p[2 * h + 1, t] = got[:, tall:]

    def compute(c):
        if c:
            @pl.loop(0, c)
            def _(i):
                scale(i)
                tiles(c, c * c + i)

        scale(c)

        @pl.loop(0, c + 1)
        def _(i):
            tiles(i, c * c + c + i)

        for b in range(2):
            first(c, b).start()

    def halve(c):
        for b in range(2):
            first(c, b).wait_recv()

        @pl.loop(c * c, (c + 1) * (c + 1))
        def _(t):
            p[far, t] += s1[1 - half, t]

        second(c).start()

        @pl.loop(c * c, (c + 1) * (c + 1))
        def _(t):
            p[z, t] += s1[half, t]

    def place(c1, c2, t):
        done = p[z, t] + s2[t]
        for i in range(n_pair):
            row = pl.multiple_of(i * chunks * step + c1 * step, step)
            for j in range(n_pair):
                column = (j * chunks + c2) * step
                o_ref[pl.ds(row, step), column : column + step] = done[
                    i * step : (i + 1) * step, j * step : (j + 1) * step
                ]

    def finish(c):
        second(c).wait_recv()
        if c:
            @pl.loop(0, c)
            def _(i):
                place(i, c, c * c + i)

        for i in range(c + 1):
            place(c, i, c * c + c + i)

    for k in range(1, n_pair):
        e_copy(k, True).start()
    start_z(0)
    start_z(1)
    own = pltpu.make_async_copy(x_ref.at[z], g.at[:, mine, z], ls)
    own.start()
    for c in range(chunks):
        arrived(c, 0)
    weigh()
    own.wait()
    for c in range(chunks + 1):
        if c < chunks:
            for j in range(1, n_pair):
                arrived(c, j)
            start_z(c + 2)
        if c > 1:
            halve(c - 2)
        if c:
            for j in range(n_pair):
                crossed(c - 1, j)
            complete(c - 1)
            compute(c - 1)
        if c > 2:
            finish(c - 3)
    halve(chunks - 1)
    finish(chunks - 2)
    finish(chunks - 1)

    for k in range(1, n_pair):
        e_copy(k, True).wait_send()
    for c in range(chunks):
        second(c).wait_send()
        for b in range(2):
            first(c, b).wait_send()
        for k in range(1, n_pair):
            z_copy(c, k, True).wait_send()
        for j in range(n_pair):
            for k in range(1, n_aux):
                x_copy(c, k, j, True).wait_send()
            for m in range(1, n_rep):
                for k in range(n_aux):
                    c_copy(c, m, k, j, True).wait_send()


def fused(pieces, eps_occ, eps_virt, freq, n_aux, n_rep):
    n_pair, chunks, step, width = pieces.shape
    tall = n_pair * step
    groups = n_aux * n_rep
    sizes = (n_pair, n_aux, n_rep, chunks, step, width)
    dma = pltpu.SemaphoreType.DMA
    return pl.pallas_call(
        functools.partial(fused_kernel, sizes),
        out_shape=jax.ShapeDtypeStruct((chunks * tall, chunks * tall), jnp.float32),
        in_specs=[
            pl.BlockSpec(memory_space=pl.ANY),
            pl.BlockSpec(memory_space=pltpu.SMEM),
            pl.BlockSpec(memory_space=pltpu.VMEM),
            pl.BlockSpec(memory_space=pltpu.SMEM),
        ],
        out_specs=pl.BlockSpec(memory_space=pltpu.VMEM),
        scratch_shapes=[
            pltpu.VMEM((chunks, groups, n_pair, step, width), jnp.bfloat16),
            pltpu.VMEM((groups, chunks * chunks, tall, tall), jnp.float32),
            pltpu.VMEM((2, chunks * chunks, tall, tall), jnp.float32),
            pltpu.VMEM((chunks * chunks, tall, tall), jnp.float32),
            pltpu.VMEM((tall, width), jnp.bfloat16),
            pltpu.VMEM((n_pair, 1, width // n_pair), jnp.float32),
            pltpu.VMEM((1, width), jnp.float32),
            dma((chunks, n_pair)),
            dma((chunks, n_pair)),
            dma((chunks, n_aux, n_pair)),
            dma((chunks, n_aux, n_pair)),
            dma((chunks, n_rep, n_aux, n_pair)),
            dma((chunks, n_rep, n_aux, n_pair)),
            dma,
            dma((chunks, 2)),
            dma((chunks, 2)),
            dma((chunks,)),
            dma((chunks,)),
            dma((n_pair,)),
            dma((n_pair,)),
        ],
        compiler_params=pltpu.CompilerParams(
            collective_id=1, has_side_effects=True, vmem_limit_bytes=60 * 2**20
        ),
    )(pieces, eps_occ, eps_virt[None, :], freq)


def local(mesh, three_center, eps_occ, eps_virt, freq):
    n_pair, n_aux, n_rep = (mesh.shape[name] for name in ("pair", "aux", "rep"))
    rows, n_occ, n_virt = three_center.shape
    if n_pair == n_occ == n_aux * n_rep == 4 and rows % 32 == 0:
        return whole_kernel(n_aux, n_rep, three_center, eps_occ, eps_virt, freq)
    return staged(n_pair, n_aux, n_rep, three_center, eps_occ, eps_virt, freq)


def whole_kernel(n_aux, n_rep, three_center, eps_occ, eps_virt, freq):
    rows, n_pair, n_virt = three_center.shape
    pieces = three_center.transpose(1, 0, 2).reshape(n_pair, rows // 32, 32, n_virt)
    return fused(pieces, eps_occ, eps_virt, freq, n_aux, n_rep)


def staged(n_pair, n_aux, n_rep, three_center, eps_occ, eps_virt, freq):
    rows, n_occ, n_virt = three_center.shape
    parts = n_pair // n_occ
    width = n_virt // parts
    every_virt = lax.all_gather(eps_virt, "pair", axis=0, tiled=True)
    pieces = three_center.reshape(rows, n_pair, width).transpose(1, 0, 2)
    gathered = gather(pieces, n_aux, n_rep)

    z = lax.axis_index("pair")
    virt = lax.dynamic_slice_in_dim(every_virt, lax.rem(z, parts) * width, width)
    occ = lax.dynamic_index_in_dim(eps_occ, z // parts, keepdims=False)
    excite = virt - occ
    weight = 2.0 * excite / (excite * excite + freq[0] * freq[0])
    plain = gathered.reshape(n_aux * n_rep, n_pair * rows, width)
    mine = lax.axis_index("aux") * n_rep + lax.axis_index("rep")
    own = lax.dynamic_index_in_dim(plain, mine, keepdims=False)
    scaled = (own.astype(jnp.float32) * weight[None, :]).astype(jnp.bfloat16)
    partial_sums = lax.dot_general(
        scaled,
        plain.reshape(-1, width),
        (((1,), (1,)), ((), ())),
        preferred_element_type=jnp.float32,
    )
    return lax.psum_scatter(partial_sums, "pair", scatter_dimension=1, tiled=True)


def solution(mesh):
    return jax.shard_map(
        functools.partial(local, mesh),
        mesh=mesh,
        in_specs=(
            P(("grp", "aux", "rep", "pair"), None, None),
            P("grp"),
            P(("grp", "pair")),
            P("grp"),
        ),
        out_specs=P(("grp", "aux", "rep"), "pair"),
        check_vma=False,
    )
```
